32 devices in a mesh: run: 8 (over z, y), rep: 4 (over x, core).
Axes of the slice: x: 2, y: 2, z: 4, core: 2. Of those that a mesh axis runs over, the one named last changes fastest.
Arguments:
- edge_feats: bfloat16 [4, 16384, 1280], P('rep', 'run'), may hold values from -6 to 6
- edge_grads: bfloat16 [4, 16384, 640], P('rep', 'run'), may hold values from -0.059814453 to 0.059814453
- edge_system: int32 [4, 16384], P('rep', 'run'), may hold values from 0 to 5, as said below
- edge_count: int32 [4, 8], P('rep', 'run'), may hold values from 1025 to 2048
- coef: float32 [4, 6, 32], P('rep'), may hold values from 0.05 to 1
- weights: float32 [32, 1280, 640], P('rep', 'run'), may hold values from -0.15625 to 0.15625
- first_moment: float32 [32, 1280, 640], P('rep', 'run'), may hold values from -6 to 6
- second_moment: float32 [32, 1280, 640], P('rep', 'run'), may hold values from 1 to 10
Outputs:
- new_weights: float32 [32, 1280, 640], P('rep', 'run')
- new_first: float32 [32, 1280, 640], P('rep', 'run')
- new_second: float32 [32, 1280, 640], P('rep', 'run')
- merged_next: bfloat16 [4, 6, 1280, 640], P('rep', None, 'run')
The draws below stay inside these ranges and needn't reach their ends.
Inputs may be any that keep to these rules, and one draw needn't show every extreme that they name: `edge_system`: along each replica's rows the system never falls; every system number appears; the live rows of one device belong to one or two systems, two on some device in every draw.
All inputs are finite; a program needn't handle non-finite values.
Results may differ from the reference program's by a relative error of at most 0.001.
The reference program's roundings to bfloat16 on the way (of `rounded`) count: a program that leaves them out, or rounds other values in their place, can miss the bound.
Values may be sent and summed in bfloat16 or wider, within the bound.
A program may use at most 128 MiB of HBM per device.

```python
import math
import jax
import jax.numpy as jnp
from jax import lax

DIN = 1280
DOUT = 640
EXPERTS = 32
NSYS = 6
ROWS = 2048
EDGES = 16384
N_RUN = 8
N_REP = 4


def draw_edge_system(key, part):

    def replica_ids(replica_key):
        key_block, key_offset = jax.random.split(replica_key)
        blocks = jnp.sort(jax.random.randint(key_block, (NSYS - 1,), 0, N_RUN - NSYS + 1))
        offsets = jnp.sort(jax.random.randint(key_offset, (NSYS - 1,), 1, ROWS // 2 + 1))
        bounds = (jnp.arange(1, NSYS) + blocks) * ROWS + offsets
        position = jnp.arange(N_RUN * ROWS)
        return jnp.sum((position[:, None] >= bounds[None, :]).astype(jnp.int32), axis=1).astype(jnp.int32)
    replica_keys = jax.random.split(key, N_REP)
    return jax.vmap(replica_ids)(replica_keys)


def place_ends(values, rng, smallest, top_value):
    dims = values.shape
    place = [jax.random.randint(jax.random.fold_in(rng, axis), (), 0, dims[axis]) for axis in range(len(dims))]
    values = values.at[tuple(place)].set(smallest)
    longest = dims.index(max(dims))
    place[longest] = (place[longest] + 1) % dims[longest]
    return values.at[tuple(place)].set(top_value)


def block_scale(stream_key, shape, shards, low, high):
    level, own = 1.0, jax.random.fold_in(stream_key, 6)
    for axis_at, shards_of in shards:
        draws = jnp.exp(jax.random.uniform(jax.random.fold_in(own, axis_at), (shards_of,), jnp.float32, low / len(shards), high / len(shards)))
        level = level * jnp.repeat(draws, shape[axis_at] // shards_of).reshape([-1 if axis == axis_at else 1 for axis in range(len(shape))])
    return level


def scatter_about(rng, extent, scale, reach, cuts=(), dtype=jnp.bfloat16):
    result = jax.random.normal(rng, extent, jnp.float32) * scale
    if len(cuts) > 0:
        result = block_scale(rng, extent, cuts, -0.22, 0.18) * result
    return jnp.clip(result, min=-reach, max=reach).astype(dtype)


def setup_inputs(seed: int = 0) -> dict:
    keys = jax.random.split(jax.random.key(seed), 9)
    edge_feats = scatter_about(keys[0], (N_REP, EDGES, DIN), 1.0, 6.0, ((0, 4), (1, 8)))
    edge_grads = scatter_about(keys[1], (N_REP, EDGES, DOUT), 0.01, 0.059814453, ((0, 4), (1, 8)))
    edge_system = draw_edge_system(jax.random.fold_in(keys[8], 71), 0)
    edge_count = place_ends(jax.random.randint(keys[3], (N_REP, N_RUN), ROWS // 2 + 1, ROWS + 1), jax.random.fold_in(keys[3], 1), ROWS // 2 + 1, ROWS).astype(jnp.int32)
    coef = jnp.clip(jnp.exp(math.log(1.0) - 2.9957323 * jax.random.uniform(keys[4], (N_REP, NSYS, EXPERTS), jnp.float32) ** block_scale(keys[4], (N_REP, NSYS, EXPERTS), ((0, 4),), -0.2, 0.2)), 0.05, 1.0)
    weights = scatter_about(keys[5], (EXPERTS, DIN, DOUT), DIN ** -0.5, 0.15625, ((0, 4), (1, 8)), jnp.float32)
    first_moment = scatter_about(keys[6], (EXPERTS, DIN, DOUT), 1.0, 6.0, ((0, 4), (1, 8)), jnp.float32)
    second_moment = jnp.clip(jnp.exp(math.log(10.0) - 2.3025851 * jax.random.uniform(keys[7], (EXPERTS, DIN, DOUT), jnp.float32) ** block_scale(keys[7], (EXPERTS, DIN, DOUT), ((0, 4), (1, 8)), -0.2, 0.2)), 1.0, 10.0)
    return {"edge_feats": edge_feats, "edge_grads": edge_grads, "edge_system": edge_system, "edge_count": edge_count, "coef": coef, "weights": weights, "first_moment": first_moment, "second_moment": second_moment}


def system_sums(feats, grads, system, counts):
    feat_blocks = feats.reshape(N_RUN, ROWS, DIN)
    grad_blocks = grads.reshape(N_RUN, ROWS, DOUT)
    sys_blocks = system.reshape(N_RUN, ROWS)

    def device_step(total, item):
        feat_rows, grad_rows, sys_rows, live_count = item
        live = jnp.arange(ROWS) < live_count
        first = sys_rows[0]
        last = lax.dynamic_index_in_dim(sys_rows, live_count - 1, 0, keepdims=False)
        left = feat_rows.astype(jnp.float32)

        def slot(offset):
            keep = live & (sys_rows == first + offset)
            right = jnp.where(keep[:, None], grad_rows.astype(jnp.float32), jnp.float32(0.0))
            return lax.dot_general(left, right, (((0,), (0,)), ((), ())), precision=lax.Precision.HIGHEST)
        lower = slot(0)
        upper = lax.cond(last > first, lambda: slot(1), lambda: jnp.zeros_like(lower))
        total = total.at[first].add(lower)
        total = total.at[jnp.minimum(first + 1, NSYS - 1)].add(upper)
        return (total, None)
    start = jnp.zeros((NSYS, DIN, DOUT), jnp.float32)
    total, _ = lax.scan(device_step, start, (feat_blocks, grad_blocks, sys_blocks, counts))
    return total

def reference(edge_feats, edge_grads, edge_system, edge_count, coef, weights, first_moment, second_moment):

    def replica_step(total, item):
        feats, grads, system, counts, group_coef = item
        sums = system_sums(feats, grads, system, counts)
        mixed = jnp.einsum('se,sio->eio', group_coef, sums, precision=lax.Precision.HIGHEST)
        return (total + mixed, None)
    start = jnp.zeros((EXPERTS, DIN, DOUT), jnp.float32)
    expert_grad, _ = lax.scan(replica_step, start, (edge_feats, edge_grads, edge_system, edge_count, coef))
    new_first = 0.9 * first_moment + 0.1 * expert_grad
    new_second = 0.999 * second_moment + 0.001 * expert_grad * expert_grad
    corr_first = 1.0 - 0.9 ** 10
    corr_second = 1.0 - 0.999 ** 10
    new_weights = weights - 0.01 * (new_first / corr_first) / (jnp.sqrt(new_second / corr_second) + 1e-08)
    rounded = lax.optimization_barrier(new_weights.astype(jnp.bfloat16))
    flat = rounded.astype(jnp.float32).reshape(EXPERTS, DIN * DOUT)
    merged = jnp.einsum('rse,ek->rsk', coef, flat, precision=lax.Precision.HIGHEST)
    merged_next = merged.reshape(N_REP, NSYS, DIN, DOUT).astype(jnp.bfloat16)
    return (new_weights, new_first, new_second, merged_next)
```

```python
import functools
import jax
import jax.numpy as jnp
from jax import lax
from jax.experimental import pallas as pl
from jax.experimental.pallas import tpu as pltpu
from jax.sharding import PartitionSpec as P

MESH = pl.DeviceIdType.MESH
LANES = 128
DEPTH = 256
AHEAD = 2


def step_kernel(
    n_run, n_rep, nsys, held, units, hr, per_block,
    coef, count, system, feats, grads, weights, moment1, moment2,
    wbuf, fbuf, sbuf, mbuf,
    fin, fturn, gin, gpair, out_slots, land, sums, rounded,
    mark, mark_land, coef_mine, coef_land,
    edge_sem, in_sem, own_sem, a2a_send, a2a_recv, mark_send, mark_recv,
    coef_send, coef_recv, x_send, x_recv, pair_send, pair_recv,
):
    me = lax.axis_index("run")
    rep = lax.axis_index("rep")
    partner = rep + 1 - 2 * lax.rem(rep, 2)
    n_x = n_rep // 2
    n_edge, din = fin.shape
    steps = n_edge // DEPTH
    local = din // n_run
    splits = local // hr
    n_units = len(units)
    f32, bf16 = jnp.float32, jnp.bfloat16

    barrier = pltpu.get_barrier_semaphore()
    for o in range(1, n_run):
        pl.semaphore_signal(
            barrier, inc=1, device_id={"run": jnp.bitwise_xor(me, o)}, device_id_type=MESH
        )
    for o in range(1, n_rep):
        pl.semaphore_signal(
            barrier, inc=1, device_id={"rep": lax.rem(rep + o, n_rep)}, device_id_type=MESH
        )

    edge_loads = []
    for k in range(steps):
        rows = pl.ds(k * DEPTH, DEPTH)
        pair = (
            pltpu.make_async_copy(feats.at[0, rows], fin.at[rows], edge_sem.at[0, k]),
            pltpu.make_async_copy(grads.at[0, rows], gin.at[rows], edge_sem.at[1, k]),
        )
        for copy in pair:
            copy.start()
        edge_loads.append(pair)
    loads = [
        pltpu.make_async_copy(src, dst, in_sem.at[i])
        for i, (src, dst) in enumerate(((weights, wbuf), (moment1, fbuf), (moment2, sbuf)))
    ]
    for load in loads:
        load.start()

    ids = system[...]
    first = jnp.min(ids, axis=1, keepdims=True)
    live = lax.broadcasted_iota(jnp.int32, ids.shape, 1) < count[0, 0]
    split = jnp.sum((live & (ids == first)).astype(jnp.int32), axis=1, keepdims=True)
    end = jnp.sum((live & (ids <= first + 1)).astype(jnp.int32), axis=1, keepdims=True)
    at = lax.broadcasted_iota(jnp.int32, mark.shape, 0)
    mark[...] = (at == first + 1).astype(f32)

    def spell(i, carry):
        r = lax.div(i, nsys * held)
        j = lax.rem(i, nsys * held)
        value = coef[0, lax.div(j, held), r * held + lax.rem(j, held)]
        coef_mine[r, pl.ds(j, 1), :] = jnp.full((1, LANES), value, f32)
        return carry

    lax.fori_loop(0, n_rep * nsys * held, spell, 0)

    started = []

    def send(src, dst, send_sem, recv_sem, device):
        copy = pltpu.make_async_remote_copy(
            src_ref=src, dst_ref=dst, send_sem=send_sem, recv_sem=recv_sem,
            device_id=device, device_id_type=MESH,
        )
        copy.start()
        started.append(copy)
        return copy

    def mask(c):
        for k in range(steps):
            rows = pl.ds(k * DEPTH, DEPTH)
            if c == 0:
                for copy in edge_loads[k]:
                    copy.wait()
                fturn[:, k * DEPTH : (k + 1) * DEPTH] = fin[rows, :].T
            part = gin[rows, c * LANES : (c + 1) * LANES].astype(f32)
            place = lax.broadcasted_iota(jnp.int32, part.shape, 0) + k * DEPTH
            low = jnp.where(place < split, part, 0.0)
            high = jnp.where((place >= split) & (place < end), part, 0.0)
            gpair[rows, :LANES] = low.astype(bf16)
            gpair[rows, LANES:] = high.astype(bf16)

    def multiply(c):
        size = per_block * local

        def step(i, carry):
            base = pl.multiple_of(i * size, size)
            block = jnp.dot(
                fturn[pl.ds(base, size), :], gpair[...], preferred_element_type=f32
            )
            for p in range(per_block):
                for h in range(splits):
                    rows = slice(p * local + h * hr, p * local + (h + 1) * hr)
                    u = c * splits + h
                    owner = i * per_block + p
                    out_slots[u, owner, 0] = block[rows, :LANES].astype(bf16)
                    out_slots[u, owner, 1] = block[rows, LANES:].astype(bf16)
            return carry

        lax.fori_loop(0, n_run // per_block, step, 0)

    pieces = []

    def scatter(u):
        own = pltpu.make_async_copy(out_slots.at[u, me], land.at[u, me], own_sem.at[u])
        own.start()
        pieces.append([own])
        for o in range(1, n_run):
            dest = jnp.bitwise_xor(me, o)
            pieces[u].append(
                send(out_slots.at[u, dest], land.at[u, me], a2a_send.at[u, o - 1],
                     a2a_recv.at[u, o - 1], {"run": dest})
            )

    marks, coefs = [], []
    mask(0)
    multiply(0)
    pl.semaphore_wait(barrier, n_run + n_rep - 2)
    for o in range(1, n_run):
        marks.append(
            send(mark, mark_land.at[me], mark_send.at[o - 1], mark_recv.at[o - 1],
                 {"run": jnp.bitwise_xor(me, o)})
        )
    for o in range(1, n_rep):
        dest = lax.rem(rep + o, n_rep)
        coefs.append(
            send(coef_mine.at[dest], coef_land.at[rep], coef_send.at[o - 1],
                 coef_recv.at[o - 1], {"rep": dest})
        )
    for u in range(splits):
        scatter(u)
    if n_units > splits:
        mask(1)
        multiply(1)
    for u in range(splits, AHEAD):
        scatter(u)

    mark_land[me] = mark[...]
    coef_land[rep] = coef_mine[rep]

    group = 16 if hr % 16 == 0 else hr

    def tiles(body):
        def step(i, carry):
            body(pl.multiple_of(i * group, group))
            return carry

        lax.fori_loop(0, hr // group, step, 0)

    def spread(buf, kind, u):
        direct = send(buf.at[u, rep], buf.at[u, rep], pair_send.at[kind, u, 0],
                      pair_recv.at[kind, u, 0], {"rep": partner})
        across = [
            send(buf.at[u, rep], buf.at[u, rep], x_send.at[kind, u, j - 1],
                 x_recv.at[kind, u, j - 1], {"rep": lax.rem(rep + 2 * j, n_rep)})
            for j in range(1, n_x)
        ]
        return [direct], across

    def relay(buf, kind, u, moving):
        near, across = moving
        for j in range(1, n_x):
            across[j - 1].wait_recv()
            slot = lax.rem(rep + n_rep - 2 * j, n_rep)
            near.append(
                send(buf.at[u, slot], buf.at[u, slot], pair_send.at[kind, u, j],
                     pair_recv.at[kind, u, j], {"rep": partner})
            )

    def collect(moving):
        for copy in moving[0]:
            copy.wait_recv()

    def sum_systems(u):
        def body(row):
            rows = pl.ds(row, group)
            total = [jnp.zeros((group, LANES), f32)] * nsys
            for k in range(n_run):
                low = land[u, k, 0, rows, :].astype(f32)
                high = land[u, k, 1, rows, :].astype(f32)
                for s in range(nsys):
                    total[s] = (
                        total[s]
                        + mark_land[k, s + 1 : s + 2, :] * low
                        + mark_land[k, s : s + 1, :] * high
                    )
            for s in range(nsys):
                sums[u, rep, s, rows, :] = total[s].astype(bf16)

        tiles(body)

    def update(u):
        base, lane = units[u]

        def body(row):
            rows, lanes = pl.ds(row, group), slice(lane, lane + LANES)
            place = pl.ds(pl.multiple_of(base + row, 8), group)
            grad = [jnp.zeros((group, LANES), f32)] * held
            for r in range(n_rep):
                for s in range(nsys):
                    part = sums[u, r, s, rows, :].astype(f32)
                    for e in range(held):
                        at = s * held + e
                        grad[e] = grad[e] + coef_land[r, at : at + 1, :] * part
            for e in range(held):
                new_first = 0.9 * fbuf[e, place, lanes] + 0.1 * grad[e]
                new_second = 0.999 * sbuf[e, place, lanes] + 0.001 * grad[e] * grad[e]
                corr_first = 1.0 - 0.9**10
                corr_second = 1.0 - 0.999**10
                new_weights = wbuf[e, place, lanes] - (0.01 / corr_first) * new_first / (
                    jnp.sqrt(new_second * (1.0 / corr_second)) + 1e-08
                )
                fbuf[e, place, lanes] = new_first
                sbuf[e, place, lanes] = new_second
                wbuf[e, place, lanes] = new_weights
                rounded[u, rep, e, rows, :] = new_weights.astype(bf16)

        tiles(body)

    def merge(u):
        base, lane = units[u]

        def body(row):
            rows = pl.ds(row, group)
            place = pl.ds(pl.multiple_of(base + row, group), group)
            total = [jnp.zeros((group, LANES), f32)] * nsys
            for r in range(n_rep):
                for e in range(held):
                    part = rounded[u, r, e, rows, :].astype(f32)
                    for s in range(nsys):
                        at = s * held + e
                        total[s] = total[s] + coef_mine[r, at : at + 1, :] * part
            for s in range(nsys):
                mbuf[s, place, lane : lane + LANES] = total[s].astype(bf16)

        tiles(body)

    for copy in marks:
        copy.wait_recv()
    for copy in coefs:
        copy.wait_recv()
    for load in loads:
        load.wait()

    moved_sums, moved_new = {}, {}
    for t in range(n_units + 2):
        if t < n_units:
            pieces[t][0].wait()
            for copy in pieces[t][1:]:
                copy.wait_recv()
        if t + AHEAD < n_units:
            scatter(t + AHEAD)
        if 1 <= t <= n_units:
            relay(sums, 0, t - 1, moved_sums[t - 1])
        if t < n_units:
            sum_systems(t)
            moved_sums[t] = spread(sums, 0, t)
        if t >= 2:
            relay(rounded, 1, t - 2, moved_new[t - 2])
        if 1 <= t <= n_units:
            collect(moved_sums[t - 1])
            update(t - 1)
            moved_new[t - 1] = spread(rounded, 1, t - 1)
        if t >= 2:
            collect(moved_new[t - 2])
            merge(t - 2)
        c = t // splits + 2
        if t % splits == 0 and c * splits < n_units:
            mask(c)
            multiply(c)
    for copy in started:
        copy.wait_send()


def store_kernel(w, f, s, m, w_out, f_out, s_out, m_out, sems):
    copies = [
        pltpu.make_async_copy(src, dst, sems.at[i])
        for i, (src, dst) in enumerate(((w, w_out), (f, f_out), (s, s_out), (m, m_out.at[0])))
    ]
    for copy in copies:
        copy.start()
    for copy in copies:
        copy.wait()


def on_device(
    n_run, n_rep,
    edge_feats, edge_grads, edge_system, edge_count, coef, weights, first_moment, second_moment
):
    _, nsys, experts = coef.shape
    held, local, dout = weights.shape
    _, n_edge, din = edge_feats.shape
    hr = local // 2 if local % 32 == 0 else local
    units = [(row, lane) for lane in range(0, dout, LANES) for row in range(0, local, hr)]
    n_units = len(units)
    per_block = 1
    while per_block * local % 16:
        per_block *= 2

    bf16, f32 = jnp.bfloat16, jnp.float32
    dma = pltpu.SemaphoreType.DMA
    n_x = n_rep // 2
    mark_rows = -(-(nsys + 1) // 8) * 8
    anywhere = pl.BlockSpec(memory_space=pl.ANY)
    vmem = pl.BlockSpec(memory_space=pltpu.VMEM)
    smem = pl.BlockSpec(memory_space=pltpu.SMEM)
    kept = pltpu.VMEM(weights.shape, f32)
    outs = pl.pallas_call(
        functools.partial(step_kernel, n_run, n_rep, nsys, held, units, hr, per_block),
        out_shape=(kept, kept, kept, pltpu.VMEM((nsys, local, dout), bf16)),
        in_specs=[smem, smem, vmem] + [anywhere] * 5,
        out_specs=(vmem,) * 4,
        scratch_shapes=[
            pltpu.VMEM((n_edge, din), bf16),
            pltpu.VMEM((din, n_edge), bf16),
            pltpu.VMEM((n_edge, dout), bf16),
            pltpu.VMEM((n_edge, 2 * LANES), bf16),
            pltpu.VMEM((n_units, n_run, 2, hr, LANES), bf16),
            pltpu.VMEM((n_units, n_run, 2, hr, LANES), bf16),
            pltpu.VMEM((n_units, n_rep, nsys, hr, LANES), bf16),
            pltpu.VMEM((n_units, n_rep, held, hr, LANES), bf16),
            pltpu.VMEM((mark_rows, LANES), f32),
            pltpu.VMEM((n_run, mark_rows, LANES), f32),
            pltpu.VMEM((n_rep, nsys * held, LANES), f32),
            pltpu.VMEM((n_rep, nsys * held, LANES), f32),
            dma((2, n_edge // DEPTH)),
            dma((3,)),
            dma((n_units,)),
            dma((n_units, n_run - 1)),
            dma((n_units, n_run - 1)),
            dma((n_run - 1,)),
            dma((n_run - 1,)),
            dma((n_rep - 1,)),
            dma((n_rep - 1,)),
            dma((2, n_units, n_x)),
            dma((2, n_units, n_x)),
            dma((2, n_units, n_x)),
            dma((2, n_units, n_x)),
        ],
        compiler_params=pltpu.CompilerParams(
            collective_id=0, has_side_effects=True, vmem_limit_bytes=46 * 1024 * 1024
        ),
        name="exchange_step",
    )(coef, edge_count, edge_system, edge_feats, edge_grads, weights, first_moment, second_moment)
    block = jax.ShapeDtypeStruct(weights.shape, f32)
    return pl.pallas_call(
        store_kernel,
        out_shape=(block, block, block, jax.ShapeDtypeStruct((1, nsys, local, dout), bf16)),
        in_specs=[vmem] * 4,
        out_specs=(anywhere,) * 4,
        scratch_shapes=[dma((4,))],
        compiler_params=pltpu.CompilerParams(vmem_limit_bytes=1024 * 1024),
        name="store",
    )(*(pltpu.with_memory_space_constraint(out, pltpu.VMEM) for out in outs))


def solution(mesh):
    placed = (
        P("rep", "run", None),
        P("rep", "run", None),
        P("rep", "run"),
        P("rep", "run"),
        P("rep", None, None),
        P("rep", "run", None),
        P("rep", "run", None),
        P("rep", "run", None),
    )
    return jax.shard_map(
        functools.partial(on_device, mesh.shape["run"], mesh.shape["rep"]),
        mesh=mesh,
        in_specs=placed,
        out_specs=(
            P("rep", "run", None),
            P("rep", "run", None),
            P("rep", "run", None),
            P("rep", None, "run", None),
        ),
        check_vma=False,
    )
```

```python
import functools
import jax
import jax.numpy as jnp
from jax import lax
from jax.experimental import pallas as pl
from jax.experimental.pallas import tpu as pltpu
from jax.sharding import PartitionSpec as P

MESH = pl.DeviceIdType.MESH
LANES = 128
DEPTH = 256


def step_kernel(
    n_run, n_rep, nsys, held, units, bands,
    coef, count, system, feats, grads, weights, moment1, moment2,
    wbuf, fbuf, sbuf, mbuf,
    fin, fturn, gin, gpair, out_slots, land, sums, rounded,
    mark, mark_land, coef_mine, coef_land,
    edge_sem, in_sem, own_sem, a2a_send, a2a_recv, mark_send, mark_recv,
    coef_send, coef_recv, x_send, x_recv, pair_send, pair_recv,
):
    me = lax.axis_index("run")
    rep = lax.axis_index("rep")
    partner = rep + 1 - 2 * lax.rem(rep, 2)
    n_x = n_rep // 2
    n_edge, din = fin.shape
    steps = n_edge // DEPTH
    local = din // n_run
    n_units = len(units)
    f32, bf16 = jnp.float32, jnp.bfloat16

    barrier = pltpu.get_barrier_semaphore()
    for o in range(1, n_run):
        pl.semaphore_signal(
            barrier, inc=1, device_id={"run": jnp.bitwise_xor(me, o)}, device_id_type=MESH
        )
    for o in range(1, n_rep):
        pl.semaphore_signal(
            barrier, inc=1, device_id={"rep": lax.rem(rep + o, n_rep)}, device_id_type=MESH
        )

    edge_loads = []
    for k in range(steps):
        rows = pl.ds(k * DEPTH, DEPTH)
        pair = (
            pltpu.make_async_copy(feats.at[0, rows], fin.at[rows], edge_sem.at[0, k]),
            pltpu.make_async_copy(grads.at[0, rows], gin.at[rows], edge_sem.at[1, k]),
        )
        for copy in pair:
            copy.start()
        edge_loads.append(pair)
    loads = [
        pltpu.make_async_copy(src, dst, in_sem.at[i])
        for i, (src, dst) in enumerate(((weights, wbuf), (moment1, fbuf), (moment2, sbuf)))
    ]

    ids = system[...]
    first = jnp.min(ids, axis=1, keepdims=True)
    live = lax.broadcasted_iota(jnp.int32, ids.shape, 1) < count[0, 0]
    split = jnp.sum((live & (ids == first)).astype(jnp.int32), axis=1, keepdims=True)
    end = jnp.sum((live & (ids <= first + 1)).astype(jnp.int32), axis=1, keepdims=True)
    at = lax.broadcasted_iota(jnp.int32, mark.shape, 0)
    mark[...] = (at == first + 1).astype(f32)

    def spell(i, carry):
        r = lax.div(i, nsys * held)
        j = lax.rem(i, nsys * held)
        value = coef[lax.div(j, held), 0, r * held + lax.rem(j, held)]
        coef_mine[r, pl.ds(j, 1), :] = jnp.full((1, LANES), value, f32)
        return carry

    lax.fori_loop(0, n_rep * nsys * held, spell, 0)

    started = []

    def send(src, dst, send_sem, recv_sem, device):
        copy = pltpu.make_async_remote_copy(
            src_ref=src, dst_ref=dst, send_sem=send_sem, recv_sem=recv_sem,
            device_id=device, device_id_type=MESH,
        )
        copy.start()
        started.append(copy)
        return copy

    def mask(c):
        for k in range(steps):
            rows = pl.ds(k * DEPTH, DEPTH)
            if c == 0:
                for copy in edge_loads[k]:
                    copy.wait()
                turned = fin[rows, :].T
                for at, size in bands:
                    for owner in range(n_run):
                        row = n_run * at + owner * size
                        fturn[row : row + size, k * DEPTH : (k + 1) * DEPTH] = turned[
                            owner * local + at : owner * local + at + size
                        ]
            part = gin[rows, c * LANES : (c + 1) * LANES].astype(f32)
            place = lax.broadcasted_iota(jnp.int32, part.shape, 0) + k * DEPTH
            low = jnp.where(place < split, part, 0.0)
            high = jnp.where((place >= split) & (place < end), part, 0.0)
            gpair[rows, :LANES] = low.astype(bf16)
            gpair[rows, LANES:] = high.astype(bf16)

    def multiply(c, at, size):
        block = jnp.dot(
            fturn[n_run * at : n_run * (at + size), :], gpair[...], preferred_element_type=f32
        )
        for owner in range(n_run):
            rows = slice(owner * size, (owner + 1) * size)
            out_slots[c, owner, 0, at : at + size] = block[rows, :LANES].astype(bf16)
            out_slots[c, owner, 1, at : at + size] = block[rows, LANES:].astype(bf16)

    pieces = []

    def part_of(buf, u, *at):
        c, row, size = units[u]
        return buf.at[(c, *at, slice(None), pl.ds(row, size))]

    def scatter(u):
        own = pltpu.make_async_copy(
            part_of(out_slots, u, me), part_of(land, u, me), own_sem.at[u]
        )
        own.start()
        pieces.append([own])
        for o in range(n_run - 1, 0, -1):
            dest = jnp.bitwise_xor(me, o)
            pieces[u].append(
                send(part_of(out_slots, u, dest), part_of(land, u, me), a2a_send.at[u, o - 1],
                     a2a_recv.at[u, o - 1], {"run": dest})
            )

    masked, done = set(), set()

    def prepare(u):
        if u in done:
            return
        done.add(u)
        c, row, size = units[u]
        if c not in masked:
            masked.add(c)
            mask(c)
        for at, rows in bands:
            if row <= at < row + size:
                multiply(c, at, rows)

    ends = [c * local + row + size for c, row, size in units]

    def due(t):
        if t >= n_units:
            return []
        reach = (ends[t] if t >= 0 else 0) + local // 2
        return [u for u in range(len(pieces), n_units) if ends[u] - units[u][2] < reach]

    marks, coefs = [], []
    prepare(0)
    for load in loads:
        load.start()
    pl.semaphore_wait(barrier, n_run + n_rep - 2)
    for o in range(1, n_run):
        marks.append(
            send(mark, mark_land.at[me], mark_send.at[o - 1], mark_recv.at[o - 1],
                 {"run": jnp.bitwise_xor(me, o)})
        )
    for o in range(1, n_rep):
        dest = lax.rem(rep + o, n_rep)
        coefs.append(
            send(coef_mine.at[dest], coef_land.at[rep], coef_send.at[o - 1],
                 coef_recv.at[o - 1], {"rep": dest})
        )
    for u in due(-1):
        prepare(u)
        scatter(u)
    for u in due(0):
        prepare(u)

    mark_land[me] = mark[...]
    coef_land[rep] = coef_mine[rep]

    def tiles(u, body):
        _, base, size = units[u]
        group = 16 if size % 16 == 0 else size
        align = 16 if size % 16 == 0 else 8

        def step(i, carry):
            body(pl.ds(pl.multiple_of(base + i * group, align), group), (group, LANES))
            return carry

        lax.fori_loop(0, size // group, step, 0)

    def spread(buf, kind, u):
        direct = send(part_of(buf, u, rep), part_of(buf, u, rep), pair_send.at[kind, u, 0],
                      pair_recv.at[kind, u, 0], {"rep": partner})
        across = [
            send(part_of(buf, u, rep), part_of(buf, u, rep), x_send.at[kind, u, j - 1],
                 x_recv.at[kind, u, j - 1], {"rep": lax.rem(rep + 2 * j, n_rep)})
            for j in range(1, n_x)
        ]
        return [direct], across

    def relay(buf, kind, u, moving):
        near, across = moving
        for j in range(1, n_x):
            across[j - 1].wait_recv()
            slot = lax.rem(rep + n_rep - 2 * j, n_rep)
            near.append(
                send(part_of(buf, u, slot), part_of(buf, u, slot), pair_send.at[kind, u, j],
                     pair_recv.at[kind, u, j], {"rep": partner})
            )

    def collect(moving):
        for copy in moving[0]:
            copy.wait_recv()

    def sum_systems(u):
        c = units[u][0]

        def body(rows, shape):
            total = [jnp.zeros(shape, f32)] * nsys
            for k in range(n_run):
                low = land[c, k, 0, rows, :].astype(f32)
                high = land[c, k, 1, rows, :].astype(f32)
                for s in range(nsys):
                    total[s] = (
                        total[s]
                        + mark_land[k, s + 1 : s + 2, :] * low
                        + mark_land[k, s : s + 1, :] * high
                    )
            for s in range(nsys):
                sums[c, rep, s, rows, :] = total[s].astype(bf16)

        tiles(u, body)

    def update(u):
        c = units[u][0]
        lanes = slice(c * LANES, (c + 1) * LANES)

        def body(rows, shape):
            grad = [jnp.zeros(shape, f32)] * held
            for r in range(n_rep):
                for s in range(nsys):
                    part = sums[c, r, s, rows, :].astype(f32)
                    for e in range(held):
                        at = s * held + e
                        grad[e] = grad[e] + coef_land[r, at : at + 1, :] * part
            for e in range(held):
                new_first = 0.9 * fbuf[e, rows, lanes] + 0.1 * grad[e]
                new_second = 0.999 * sbuf[e, rows, lanes] + 0.001 * grad[e] * grad[e]
                corr_first = 1.0 - 0.9**10
                corr_second = 1.0 - 0.999**10
                new_weights = wbuf[e, rows, lanes] - (0.01 / corr_first) * new_first / (
                    jnp.sqrt(new_second * (1.0 / corr_second)) + 1e-08
                )
                fbuf[e, rows, lanes] = new_first
                sbuf[e, rows, lanes] = new_second
                wbuf[e, rows, lanes] = new_weights
                rounded[c, rep, e, rows, :] = new_weights.astype(bf16)

        tiles(u, body)

    def merge(u):
        c = units[u][0]
        lanes = slice(c * LANES, (c + 1) * LANES)

        def body(rows, shape):
            total = [jnp.zeros(shape, f32)] * nsys
            for r in range(n_rep):
                for e in range(held):
                    part = rounded[c, r, e, rows, :].astype(f32)
                    for s in range(nsys):
                        at = s * held + e
                        total[s] = total[s] + coef_mine[r, at : at + 1, :] * part
            for s in range(nsys):
                mbuf[s, rows, lanes] = total[s].astype(bf16)

        tiles(u, body)

    for copy in marks:
        copy.wait_recv()
    for copy in coefs:
        copy.wait_recv()

    moved_sums, moved_new = {}, {}
    for t in range(n_units + 3):
        if t < n_units:
            pieces[t][0].wait()
            for copy in pieces[t][1:]:
                copy.wait_recv()
        for u in due(t):
            scatter(u)
        if 1 <= t <= n_units:
            relay(sums, 0, t - 1, moved_sums[t - 1])
        if t < n_units:
            sum_systems(t)
            moved_sums[t] = spread(sums, 0, t)
        if 1 <= t <= n_units:
            collect(moved_sums[t - 1])
            if t == 1:
                for load in loads:
                    load.wait()
            update(t - 1)
            moved_new[t - 1] = spread(rounded, 1, t - 1)
        if 2 <= t <= n_units + 1:
            relay(rounded, 1, t - 2, moved_new[t - 2])
        if t >= 3:
            collect(moved_new[t - 3])
            merge(t - 3)
        for u in due(t + 1):
            prepare(u)
    for copy in started:
        copy.wait_send()


def store_kernel(w, f, s, m, w_out, f_out, s_out, m_out, sems):
    copies = [
        pltpu.make_async_copy(src, dst, sems.at[i])
        for i, (src, dst) in enumerate(((w, w_out), (f, f_out), (s, s_out), (m, m_out.at[0])))
    ]
    for copy in copies:
        copy.start()
    for copy in copies:
        copy.wait()


def pieces_of(rows):
    if rows % 32 or rows < 128:
        return ([(0, rows)],) * 3
    half = rows // 2
    step = half // 32 * 16
    usual = [(0, half), (half, half)]
    first = [(0, step), (step, half - step), (half, half)]
    last = [(0, half), (half, half - step), (rows - step, step)]
    return first, usual, usual


def on_device(
    n_run, n_rep,
    edge_feats, edge_grads, edge_system, edge_count, coef, weights, first_moment, second_moment
):
    _, nsys, experts = coef.shape
    held, local, dout = weights.shape
    _, n_edge, din = edge_feats.shape
    chunks = dout // LANES
    first, usual, last = pieces_of(local)
    plans = [first] + [usual] * (chunks - 2) + [last]
    units = [(c, row, size) for c in range(chunks) for row, size in plans[c]]
    cuts = sorted({row for plan in plans for row, _ in plan} | {local})
    bands = [(a, b - a) for a, b in zip(cuts, cuts[1:])]
    n_units = len(units)

    bf16, f32 = jnp.bfloat16, jnp.float32
    dma = pltpu.SemaphoreType.DMA
    n_x = n_rep // 2
    mark_rows = -(-(nsys + 1) // 8) * 8
    anywhere = pl.BlockSpec(memory_space=pl.ANY)
    vmem = pl.BlockSpec(memory_space=pltpu.VMEM)
    smem = pl.BlockSpec(memory_space=pltpu.SMEM)
    kept = pltpu.VMEM(weights.shape, f32)
    outs = pl.pallas_call(
        functools.partial(step_kernel, n_run, n_rep, nsys, held, units, bands),
        out_shape=(kept, kept, kept, pltpu.VMEM((nsys, local, dout), bf16)),
        in_specs=[smem, smem, vmem] + [anywhere] * 5,
        out_specs=(vmem,) * 4,
        scratch_shapes=[
            pltpu.VMEM((n_edge, din), bf16),
            pltpu.VMEM((din, n_edge), bf16),
            pltpu.VMEM((n_edge, dout), bf16),
            pltpu.VMEM((n_edge, 2 * LANES), bf16),
            pltpu.VMEM((chunks, n_run, 2, local, LANES), bf16),
            pltpu.VMEM((chunks, n_run, 2, local, LANES), bf16),
            pltpu.VMEM((chunks, n_rep, nsys, local, LANES), bf16),
            pltpu.VMEM((chunks, n_rep, held, local, LANES), bf16),
            pltpu.VMEM((mark_rows, LANES), f32),
            pltpu.VMEM((n_run, mark_rows, LANES), f32),
            pltpu.VMEM((n_rep, nsys * held, LANES), f32),
            pltpu.VMEM((n_rep, nsys * held, LANES), f32),
            dma((2, n_edge // DEPTH)),
            dma((3,)),
            dma((n_units,)),
            dma((n_units, n_run - 1)),
            dma((n_units, n_run - 1)),
            dma((n_run - 1,)),
            dma((n_run - 1,)),
            dma((n_rep - 1,)),
            dma((n_rep - 1,)),
            dma((2, n_units, n_x)),
            dma((2, n_units, n_x)),
            dma((2, n_units, n_x)),
            dma((2, n_units, n_x)),
        ],
        compiler_params=pltpu.CompilerParams(
            collective_id=0, has_side_effects=True, vmem_limit_bytes=46 * 1024 * 1024
        ),
        name="exchange_step",
    )(coef.transpose(1, 0, 2), edge_count, edge_system, edge_feats, edge_grads, weights, first_moment, second_moment)
    block = jax.ShapeDtypeStruct(weights.shape, f32)
    return pl.pallas_call(
        store_kernel,
        out_shape=(block, block, block, jax.ShapeDtypeStruct((1, nsys, local, dout), bf16)),
        in_specs=[vmem] * 4,
        out_specs=(anywhere,) * 4,
        scratch_shapes=[dma((4,))],
        compiler_params=pltpu.CompilerParams(vmem_limit_bytes=1024 * 1024),
        name="store",
    )(*(pltpu.with_memory_space_constraint(out, pltpu.VMEM) for out in outs))


def solution(mesh):
    placed = (
        P("rep", "run", None),
        P("rep", "run", None),
        P("rep", "run"),
        P("rep", "run"),
        P("rep", None, None),
        P("rep", "run", None),
        P("rep", "run", None),
        P("rep", "run", None),
    )
    return jax.shard_map(
        functools.partial(on_device, mesh.shape["run"], mesh.shape["rep"]),
        mesh=mesh,
        in_specs=placed,
        out_specs=(
            P("rep", "run", None),
            P("rep", "run", None),
            P("rep", "run", None),
            P("rep", None, "run", None),
        ),
        check_vma=False,
    )
```

```python
import functools
import jax
import jax.numpy as jnp
from jax import lax
from jax.experimental import pallas as pl
from jax.experimental.pallas import tpu as pltpu
from jax.sharding import PartitionSpec as P

MESH = pl.DeviceIdType.MESH
LANES = 128
DEPTH = 256
LAG = 1


def step_kernel(
    n_run, n_rep, nsys, held, units, bands,
    coef, count, system, feats, grads, weights, moment1, moment2,
    wbuf, fbuf, sbuf, mbuf,
    fin, fturn, gin, gpair, out_slots, land, sums, rounded,
    mark, mark_land, coef_mine, coef_land,
    edge_sem, in_sem, own_sem, a2a_send, a2a_recv, mark_send, mark_recv,
    coef_send, coef_recv, x_send, x_recv, pair_send, pair_recv,
):
    me = lax.axis_index("run")
    rep = lax.axis_index("rep")
    partner = rep + 1 - 2 * lax.rem(rep, 2)
    n_x = n_rep // 2
    n_edge, din = fin.shape
    steps = n_edge // DEPTH
    local = din // n_run
    n_units = len(units)
    f32, bf16 = jnp.float32, jnp.bfloat16

    barrier = pltpu.get_barrier_semaphore()
    for o in range(1, n_run):
        pl.semaphore_signal(
            barrier, inc=1, device_id={"run": jnp.bitwise_xor(me, o)}, device_id_type=MESH
        )
    for o in range(1, n_rep):
        pl.semaphore_signal(
            barrier, inc=1, device_id={"rep": lax.rem(rep + o, n_rep)}, device_id_type=MESH
        )

    edge_loads = []
    for k in range(steps):
        rows = pl.ds(k * DEPTH, DEPTH)
        pair = (
            pltpu.make_async_copy(feats.at[0, rows], fin.at[rows], edge_sem.at[0, k]),
            pltpu.make_async_copy(grads.at[0, rows], gin.at[rows], edge_sem.at[1, k]),
        )
        for copy in pair:
            copy.start()
        edge_loads.append(pair)
    loads = [
        pltpu.make_async_copy(src, dst, in_sem.at[i])
        for i, (src, dst) in enumerate(((weights, wbuf), (moment1, fbuf), (moment2, sbuf)))
    ]

    ids = system[...]
    first = jnp.min(ids, axis=1, keepdims=True)
    live = lax.broadcasted_iota(jnp.int32, ids.shape, 1) < count[0, 0]
    split = jnp.sum((live & (ids == first)).astype(jnp.int32), axis=1, keepdims=True)
    end = jnp.sum((live & (ids <= first + 1)).astype(jnp.int32), axis=1, keepdims=True)
    at = lax.broadcasted_iota(jnp.int32, mark.shape, 0)
    mark[...] = (at == first + 1).astype(f32)

    def spell(i, carry):
        r = lax.div(i, nsys * held)
        j = lax.rem(i, nsys * held)
        value = coef[lax.div(j, held), 0, r * held + lax.rem(j, held)]
        coef_mine[r, pl.ds(j, 1), :] = jnp.full((1, LANES), value, f32)
        return carry

    lax.fori_loop(0, n_rep * nsys * held, spell, 0)

    started = []

    def send(src, dst, send_sem, recv_sem, device):
        copy = pltpu.make_async_remote_copy(
            src_ref=src, dst_ref=dst, send_sem=send_sem, recv_sem=recv_sem,
            device_id=device, device_id_type=MESH,
        )
        copy.start()
        started.append(copy)
        return copy

    def mask(c):
        for k in range(steps):
            rows = pl.ds(k * DEPTH, DEPTH)
            if c == 0:
                for copy in edge_loads[k]:
                    copy.wait()
                turned = fin[rows, :].T
                for at, size in bands:
                    for owner in range(n_run):
                        row = n_run * at + owner * size
                        fturn[row : row + size, k * DEPTH : (k + 1) * DEPTH] = turned[
                            owner * local + at : owner * local + at + size
                        ]
            part = gin[rows, c * LANES : (c + 1) * LANES].astype(f32)
            place = lax.broadcasted_iota(jnp.int32, part.shape, 0) + k * DEPTH
            low = jnp.where(place < split, part, 0.0)
            high = jnp.where((place >= split) & (place < end), part, 0.0)
            gpair[rows, :LANES] = low.astype(bf16)
            gpair[rows, LANES:] = high.astype(bf16)

    def multiply(c, at, size):
        block = jnp.dot(
            fturn[n_run * at : n_run * (at + size), :], gpair[...], preferred_element_type=f32
        )
        for owner in range(n_run):
            rows = slice(owner * size, (owner + 1) * size)
            out_slots[c, owner, 0, at : at + size] = block[rows, :LANES].astype(bf16)
            out_slots[c, owner, 1, at : at + size] = block[rows, LANES:].astype(bf16)

    pieces = []

    def part_of(buf, u, *at):
        c, row, size = units[u]
        return buf.at[(c, *at, slice(None), pl.ds(row, size))]

    def scatter(u):
        own = pltpu.make_async_copy(
            part_of(out_slots, u, me), part_of(land, u, me), own_sem.at[u]
        )
        own.start()
        pieces.append([own])
        for o in range(n_run - 1, 0, -1):
            dest = jnp.bitwise_xor(me, o)
            pieces[u].append(
                send(part_of(out_slots, u, dest), part_of(land, u, me), a2a_send.at[u, o - 1],
                     a2a_recv.at[u, o - 1], {"run": dest})
            )

    masked, done = set(), set()

    def prepare(u):
        if u in done:
            return
        done.add(u)
        c, row, size = units[u]
        if c not in masked:
            masked.add(c)
            mask(c)
        for at, rows in bands:
            if row <= at < row + size:
                multiply(c, at, rows)

    ends = [c * local + row + size for c, row, size in units]

    def due(t):
        if t >= n_units:
            return []
        reach = (ends[t] if t >= 0 else 0) + local // 2
        return [u for u in range(len(pieces), n_units) if ends[u] - units[u][2] < reach]

    marks, coefs = [], []
    prepare(0)
    for load in loads:
        load.start()
    pl.semaphore_wait(barrier, n_run + n_rep - 2)
    for o in range(1, n_run):
        marks.append(
            send(mark, mark_land.at[me], mark_send.at[o - 1], mark_recv.at[o - 1],
                 {"run": jnp.bitwise_xor(me, o)})
        )
    for o in range(1, n_rep):
        dest = lax.rem(rep + o, n_rep)
        coefs.append(
            send(coef_mine.at[dest], coef_land.at[rep], coef_send.at[o - 1],
                 coef_recv.at[o - 1], {"rep": dest})
        )
    for u in due(-1):
        prepare(u)
        scatter(u)
    for u in due(0):
        prepare(u)

    mark_land[me] = mark[...]
    coef_land[rep] = coef_mine[rep]

    def tiles(u, body):
        _, base, size = units[u]
        group = 16 if size % 16 == 0 else size
        align = 16 if size % 16 == 0 else 8

        def step(i, carry):
            body(pl.ds(pl.multiple_of(base + i * group, align), group), (group, LANES))
            return carry

        lax.fori_loop(0, size // group, step, 0)

    def spread(buf, kind, u):
        direct = send(part_of(buf, u, rep), part_of(buf, u, rep), pair_send.at[kind, u, 0],
                      pair_recv.at[kind, u, 0], {"rep": partner})
        across = [
            send(part_of(buf, u, rep), part_of(buf, u, rep), x_send.at[kind, u, j - 1],
                 x_recv.at[kind, u, j - 1], {"rep": lax.rem(rep + 2 * j, n_rep)})
            for j in range(1, n_x)
        ]
        return [direct], across

    def relay(buf, kind, u, moving):
        near, across = moving
        for j in range(1, n_x):
            across[j - 1].wait_recv()
            slot = lax.rem(rep + n_rep - 2 * j, n_rep)
            near.append(
                send(part_of(buf, u, slot), part_of(buf, u, slot), pair_send.at[kind, u, j],
                     pair_recv.at[kind, u, j], {"rep": partner})
            )

    def collect(moving):
        for copy in moving[0]:
            copy.wait_recv()

    def sum_systems(u):
        c = units[u][0]

        def body(rows, shape):
            total = [jnp.zeros(shape, f32)] * nsys
            for k in range(n_run):
                low = land[c, k, 0, rows, :].astype(f32)
                high = land[c, k, 1, rows, :].astype(f32)
                for s in range(nsys):
                    total[s] = (
                        total[s]
                        + mark_land[k, s + 1 : s + 2, :] * low
                        + mark_land[k, s : s + 1, :] * high
                    )
            for s in range(nsys):
                sums[c, rep, s, rows, :] = total[s].astype(bf16)

        tiles(u, body)

    def update(u):
        c = units[u][0]
        lanes = slice(c * LANES, (c + 1) * LANES)

        def body(rows, shape):
            grad = [jnp.zeros(shape, f32)] * held
            for r in range(n_rep):
                for s in range(nsys):
                    part = sums[c, r, s, rows, :].astype(f32)
                    for e in range(held):
                        at = s * held + e
                        grad[e] = grad[e] + coef_land[r, at : at + 1, :] * part
            for e in range(held):
                new_first = 0.9 * fbuf[e, rows, lanes] + 0.1 * grad[e]
                new_second = 0.999 * sbuf[e, rows, lanes] + 0.001 * grad[e] * grad[e]
                corr_first = 1.0 - 0.9**10
                corr_second = 1.0 - 0.999**10
                new_weights = wbuf[e, rows, lanes] - (0.01 / corr_first) * new_first / (
                    jnp.sqrt(new_second * (1.0 / corr_second)) + 1e-08
                )
                fbuf[e, rows, lanes] = new_first
                sbuf[e, rows, lanes] = new_second
                wbuf[e, rows, lanes] = new_weights
                rounded[c, rep, e, rows, :] = new_weights.astype(bf16)

        tiles(u, body)

    def merge(u):
        c = units[u][0]
        lanes = slice(c * LANES, (c + 1) * LANES)

        def body(rows, shape):
            total = [jnp.zeros(shape, f32)] * nsys
            for r in range(n_rep):
                for e in range(held):
                    part = rounded[c, r, e, rows, :].astype(f32)
                    for s in range(nsys):
                        at = s * held + e
                        total[s] = total[s] + coef_mine[r, at : at + 1, :] * part
            for s in range(nsys):
                mbuf[s, rows, lanes] = total[s].astype(bf16)

        tiles(u, body)

    for copy in marks:
        copy.wait_recv()
    for copy in coefs:
        copy.wait_recv()

    moved_sums, moved_new = {}, {}
    for t in range(n_units + LAG + 2):
        if t < n_units:
            pieces[t][0].wait()
            for copy in pieces[t][1:]:
                copy.wait_recv()
        for u in due(t):
            scatter(u)
        if t < n_units:
            sum_systems(t)
            moved_sums[t] = spread(sums, 0, t)
        if 1 <= t <= n_units:
            relay(sums, 0, t - 1, moved_sums[t - 1])
        if LAG <= t < n_units + LAG:
            collect(moved_sums[t - LAG])
            if t == LAG:
                for load in loads:
                    load.wait()
            update(t - LAG)
            moved_new[t - LAG] = spread(rounded, 1, t - LAG)
        if LAG + 1 <= t < n_units + LAG + 1:
            relay(rounded, 1, t - LAG - 1, moved_new[t - LAG - 1])
        if t >= LAG + 2:
            collect(moved_new[t - LAG - 2])
            merge(t - LAG - 2)
        for u in due(t + 1):
            prepare(u)
    for copy in started:
        copy.wait_send()


def store_kernel(w, f, s, m, w_out, f_out, s_out, m_out, sems):
    pairs = ((w, w_out), (f, f_out), (s, s_out), (m, m_out.at[0]))
    copies = []
    for i, (src, dst) in enumerate(pairs):
        n = src.shape[0]
        for j, (at, size) in enumerate(((0, n // 2), (n // 2, n - n // 2))):
            part = pl.ds(at, size)
            copies.append(pltpu.make_async_copy(src.at[part], dst.at[part], sems.at[i, j]))
    for copy in copies:
        copy.start()
    for copy in copies:
        copy.wait()


def pieces_of(rows):
    if rows % 32 or rows < 128:
        return ([(0, rows)],) * 3
    half = rows // 2
    step = half // 32 * 16
    usual = [(0, half), (half, half)]
    first = [(0, step), (step, half - step), (half, half)]
    last = [(0, half), (half, half - step), (rows - step, step)]
    return first, usual, usual


def on_device(
    n_run, n_rep,
    edge_feats, edge_grads, edge_system, edge_count, coef, weights, first_moment, second_moment
):
    _, nsys, experts = coef.shape
    held, local, dout = weights.shape
    _, n_edge, din = edge_feats.shape
    chunks = dout // LANES
    first, usual, last = pieces_of(local)
    plans = [first] + [usual] * (chunks - 2) + [last]
    units = [(c, row, size) for c in range(chunks) for row, size in plans[c]]
    cuts = sorted({row for plan in plans for row, _ in plan} | {local})
    bands = [(a, b - a) for a, b in zip(cuts, cuts[1:])]
    n_units = len(units)

    bf16, f32 = jnp.bfloat16, jnp.float32
    dma = pltpu.SemaphoreType.DMA
    n_x = n_rep // 2
    mark_rows = -(-(nsys + 1) // 8) * 8
    anywhere = pl.BlockSpec(memory_space=pl.ANY)
    vmem = pl.BlockSpec(memory_space=pltpu.VMEM)
    smem = pl.BlockSpec(memory_space=pltpu.SMEM)
    kept = pltpu.VMEM(weights.shape, f32)
    outs = pl.pallas_call(
        functools.partial(step_kernel, n_run, n_rep, nsys, held, units, bands),
        out_shape=(kept, kept, kept, pltpu.VMEM((nsys, local, dout), bf16)),
        in_specs=[smem, smem, vmem] + [anywhere] * 5,
        out_specs=(vmem,) * 4,
        scratch_shapes=[
            pltpu.VMEM((n_edge, din), bf16),
            pltpu.VMEM((din, n_edge), bf16),
            pltpu.VMEM((n_edge, dout), bf16),
            pltpu.VMEM((n_edge, 2 * LANES), bf16),
            pltpu.VMEM((chunks, n_run, 2, local, LANES), bf16),
            pltpu.VMEM((chunks, n_run, 2, local, LANES), bf16),
            pltpu.VMEM((chunks, n_rep, nsys, local, LANES), bf16),
            pltpu.VMEM((chunks, n_rep, held, local, LANES), bf16),
            pltpu.VMEM((mark_rows, LANES), f32),
            pltpu.VMEM((n_run, mark_rows, LANES), f32),
            pltpu.VMEM((n_rep, nsys * held, LANES), f32),
            pltpu.VMEM((n_rep, nsys * held, LANES), f32),
            dma((2, n_edge // DEPTH)),
            dma((3,)),
            dma((n_units,)),
            dma((n_units, n_run - 1)),
            dma((n_units, n_run - 1)),
            dma((n_run - 1,)),
            dma((n_run - 1,)),
            dma((n_rep - 1,)),
            dma((n_rep - 1,)),
            dma((2, n_units, n_x)),
            dma((2, n_units, n_x)),
            dma((2, n_units, n_x)),
            dma((2, n_units, n_x)),
        ],
        compiler_params=pltpu.CompilerParams(
            collective_id=0, has_side_effects=True, vmem_limit_bytes=46 * 1024 * 1024
        ),
        name="exchange_step",
    )(coef.transpose(1, 0, 2), edge_count, edge_system, edge_feats, edge_grads, weights, first_moment, second_moment)
    block = jax.ShapeDtypeStruct(weights.shape, f32)
    return pl.pallas_call(
        store_kernel,
        out_shape=(block, block, block, jax.ShapeDtypeStruct((1, nsys, local, dout), bf16)),
        in_specs=[vmem] * 4,
        out_specs=(anywhere,) * 4,
        scratch_shapes=[dma((4, 2))],
        compiler_params=pltpu.CompilerParams(vmem_limit_bytes=1024 * 1024),
        name="store",
    )(*(pltpu.with_memory_space_constraint(out, pltpu.VMEM) for out in outs))


def solution(mesh):
    placed = (
        P("rep", "run", None),
        P("rep", "run", None),
        P("rep", "run"),
        P("rep", "run"),
        P("rep", None, None),
        P("rep", "run", None),
        P("rep", "run", None),
        P("rep", "run", None),
    )
    return jax.shard_map(
        functools.partial(on_device, mesh.shape["run"], mesh.shape["rep"]),
        mesh=mesh,
        in_specs=placed,
        out_specs=(
            P("rep", "run", None),
            P("rep", "run", None),
            P("rep", "run", None),
            P("rep", None, "run", None),
        ),
        check_vma=False,
    )
```
